32 devices in a mesh: dp: 16 (over z, y, core), tensor: 2 (over x).
Axes of the slice: x: 2, y: 2, z: 4, core: 2. Of those that a mesh axis runs over, the one named last changes fastest.
Arguments:
- layer_input: bfloat16 [32768, 1024], P(('dp', 'tensor')), may hold values from -6 to 6
- attention_norm: float32 [1024], replicated, may hold values from 0.25 to 1.75
- query_weight: bfloat16 [1024, 2048], P('dp', 'tensor'), may hold values from -0.1875 to 0.1875
- key_matrix: bfloat16 [1024, 1024], P('dp', 'tensor'), may hold values from -0.1875 to 0.1875
- value_matrix: bfloat16 [1024, 1024], P('dp', 'tensor'), may hold values from -0.1875 to 0.1875
- query_norm: float32 [128], replicated, may hold values from 0.25 to 1.75
- key_norm: float32 [128], replicated, may hold values from 0.25 to 1.75
- output_weight: bfloat16 [2048, 1024], P('tensor', 'dp'), may hold values from -0.5 to 0.5
- feedforward_norm: float32 [1024], replicated, may hold values from 0.25 to 1.75
- gate_weight: bfloat16 [1024, 3072], P('dp', 'tensor'), may hold values from -0.1875 to 0.1875
- up_weight: bfloat16 [1024, 3072], P('dp', 'tensor'), may hold values from -0.1875 to 0.1875
- down_weight: bfloat16 [3072, 1024], P('tensor', 'dp'), may hold values from -0.109375 to 0.109375
- out_grad: bfloat16 [32768, 1024], P(('dp', 'tensor')), may hold values from -6 to 6
Outputs:
- layer_output: bfloat16 [32768, 1024], P(('dp', 'tensor'))
- input_grad: float32 [32768, 1024], P(('dp', 'tensor'))
- attention_norm_grad: float32 [1024], replicated
- query_weight_grad: float32 [1024, 2048], P('dp', 'tensor')
- key_weight_grad: float32 [1024, 1024], P('dp', 'tensor')
- value_weight_grad: float32 [1024, 1024], P('dp', 'tensor')
- query_norm_grad: float32 [128], replicated
- key_norm_grad: float32 [128], replicated
- output_weight_grad: float32 [2048, 1024], P('tensor', 'dp')
- feedforward_norm_grad: float32 [1024], replicated
- gate_weight_grad: float32 [1024, 3072], P('dp', 'tensor')
- up_weight_grad: float32 [1024, 3072], P('dp', 'tensor')
- down_weight_grad: float32 [3072, 1024], P('tensor', 'dp')
The draws below stay inside these ranges and needn't reach their ends.
All inputs are finite; a program needn't handle non-finite values.
Results may differ from the reference program's by a relative error of at most 0.019.
Values may be sent and summed in bfloat16 or wider, within the bound.
No kernel may reach another device: no remote copies, remote signals or barrier semaphores. Data moves between devices by JAX's collectives and lax.ppermute only.
A program may use at most 320 MiB of HBM per device.

```python
import jax
import jax.numpy as jnp
from jax import lax

MODEL_WIDTH = 1024
QUERY_HEAD_COUNT = 16
KEY_VALUE_HEADS = 8
HEAD_SIZE = 128
FF = 3072
SEQ_LEN = 2048
SEQS = 16
TOKENS = 32768


def spiked(array, rng, source, target, shards_of, factor):
    def block_of(axis_at):
        return (jnp.arange(array.shape[axis_at]) // (array.shape[axis_at] // shards_of)).reshape((-1,) + (1,) * (array.ndim - 1 - axis_at))

    near = jax.random.permutation(rng, shards_of)[block_of(target)]
    second = (block_of(target) + shards_of // 2) % shards_of
    return jnp.where((block_of(source) == near) | (block_of(source) == second), factor * array, array)


def block_levels(rng, extent, split, smallest, largest):
    loudness = 1.0
    for dim, shards_of in split:
        heights = jax.random.uniform(jax.random.fold_in(jax.random.fold_in(rng, 6), dim), (shards_of,), jnp.float32, smallest / len(split), largest / len(split))
        loudness = loudness * jnp.repeat(jnp.exp(heights), extent[dim] // shards_of).reshape((-1,) + (1,) * (len(extent) - 1 - dim))
    return loudness


def gaussian(stream_key, extent, deviation, reach, pieces=(), dtype=jnp.bfloat16):
    entries = deviation * jax.random.normal(stream_key, extent, jnp.float32)
    if pieces:
        entries = entries * block_levels(stream_key, extent, pieces, -0.22, 0.18)
    return jnp.clip(entries, -reach, reach).astype(dtype)


def heavy_noise(own_key, extent, deviation, reach, shards, heavy, dtype=jnp.bfloat16):
    drawn = deviation * jax.random.normal(own_key, extent, jnp.float32)
    if shards:
        drawn = drawn * block_levels(own_key, extent, shards, -0.22, 0.18)
    return jnp.clip(spiked(drawn, jax.random.fold_in(own_key, 3), *heavy), -reach, reach).astype(dtype)


def setup_inputs(seed: int = 0) -> dict:
    splits = jax.random.split(jax.random.key(seed), 14)
    layer_input = gaussian(splits[0], (TOKENS, MODEL_WIDTH), 1.0, 6.0, ((0, 32),))
    attention_norm = jnp.clip(1.0 + 0.15 * jax.random.normal(splits[1], (MODEL_WIDTH,), jnp.float32), 0.25, 1.75)
    query_weight = gaussian(splits[2], (MODEL_WIDTH, QUERY_HEAD_COUNT * HEAD_SIZE), MODEL_WIDTH ** -0.5, 0.1875, ((0, 16), (1, 2)))
    key_matrix = gaussian(splits[3], (MODEL_WIDTH, KEY_VALUE_HEADS * HEAD_SIZE), MODEL_WIDTH ** -0.5, 0.1875, ((0, 16), (1, 2)))
    value_matrix = gaussian(splits[4], (MODEL_WIDTH, KEY_VALUE_HEADS * HEAD_SIZE), MODEL_WIDTH ** -0.5, 0.1875, ((0, 16), (1, 2)))
    query_norm = jnp.clip(1.0 + 0.15 * jax.random.normal(splits[5], (HEAD_SIZE,), jnp.float32), 0.25, 1.75)
    key_norm = jnp.clip(1.0 + 0.15 * jax.random.normal(splits[6], (HEAD_SIZE,), jnp.float32), 0.25, 1.75)
    output_weight = gaussian(splits[7], (QUERY_HEAD_COUNT * HEAD_SIZE, MODEL_WIDTH), (QUERY_HEAD_COUNT * HEAD_SIZE // 16) ** -0.5, 0.5, ((0, 2), (1, 16)))
    feedforward_norm = jnp.clip(1.0 + 0.15 * jax.random.normal(splits[8], (MODEL_WIDTH,), jnp.float32), 0.25, 1.75)
    gate_weight = gaussian(splits[9], (MODEL_WIDTH, FF), MODEL_WIDTH ** -0.5, 0.1875, ((0, 16), (1, 2)))
    up_weight = gaussian(splits[10], (MODEL_WIDTH, FF), MODEL_WIDTH ** -0.5, 0.1875, ((0, 16), (1, 2)))
    down_weight = gaussian(splits[11], (FF, MODEL_WIDTH), FF ** -0.5, 0.109375, ((0, 2), (1, 16)))
    out_grad = heavy_noise(splits[12], (TOKENS, MODEL_WIDTH), 1.0, 6.0, ((0, 32),), (0, 1, 32, 2.75))
    return {"layer_input": layer_input, "attention_norm": attention_norm, "query_weight": query_weight, "key_matrix": key_matrix, "value_matrix": value_matrix, "query_norm": query_norm, "key_norm": key_norm, "output_weight": output_weight, "feedforward_norm": feedforward_norm, "gate_weight": gate_weight, "up_weight": up_weight, "down_weight": down_weight, "out_grad": out_grad}


@jax.custom_vjp
def lowered_precision(v):
    return lax.optimization_barrier(v.astype(jnp.bfloat16)).astype(jnp.float32)

@jax.custom_vjp
def lowered_backward(v):
    return v

def low_keep(v):
    return (lowered_precision(v), None)

def low_pass(kept, grad):
    return (grad,)

def back_keep(v):
    return (v, None)

def back_low(kept, grad):
    return (lowered_precision(grad),)
lowered_precision.defvjp(low_keep, low_pass)
lowered_backward.defvjp(back_keep, back_low)
epsilon = 1e-06
rope_base = 1000000.0
masked_score = -1e+30

def matrix_product(left, right):
    return jnp.dot(left, right, precision=lax.Precision.HIGHEST, preferred_element_type=jnp.float32)

def rms_norm(values, gain):
    return values * lax.rsqrt(lax.optimization_barrier(jnp.mean(values * values, axis=-1, keepdims=True)) + epsilon) * gain

def rope_tables(sequence_length):
    position = jnp.arange(sequence_length).astype(jnp.float32)
    inverse = jnp.power(rope_base, -jnp.arange(HEAD_SIZE // 2).astype(jnp.float32) * (2.0 / HEAD_SIZE))
    angles = position[:, None] * inverse[None, :]
    return (jnp.cos(angles), jnp.sin(angles))

def rotary(values, cosine, sine):
    half = values.shape[-1] // 2
    first = values[..., :half]
    second = values[..., half:]
    cos_wide = cosine[:, None, :]
    sin_wide = sine[:, None, :]
    return jnp.concatenate([first * cos_wide - second * sin_wide, second * cos_wide + first * sin_wide], axis=-1)

def attend_block(query_block, start, keys, values_in):
    block_slice = query_block.shape[0]
    raw = jnp.einsum('qcgd,kcd->cgqk', query_block, keys, precision=lax.Precision.HIGHEST, preferred_element_type=jnp.float32)
    scores = lowered_backward(raw * HEAD_SIZE ** (-0.5))
    rows = start + jnp.arange(block_slice).astype(jnp.int32)
    columns = jnp.arange(keys.shape[0]).astype(jnp.int32)
    allowed = columns[None, :] <= rows[:, None]
    scores = jnp.where(allowed, scores, masked_score)
    top = lax.optimization_barrier(jnp.max(scores, axis=-1, keepdims=True))
    exps = jnp.exp(scores - top)
    probs = exps / lax.optimization_barrier(jnp.sum(exps, axis=-1, keepdims=True))
    mixed = jnp.einsum('cgqk,kcd->qcgd', lowered_precision(probs), values_in, precision=lax.Precision.HIGHEST, preferred_element_type=jnp.float32)
    return lowered_precision(lowered_backward(mixed))

def layer_sequence(sequence, params):
    norm_one, query_weight, key_matrix, value_matrix, query_norm, key_norm, output_weight, norm_two, gate_weight, up_weight, down_weight = params
    sequence_length = sequence.shape[0]
    head_ratio = QUERY_HEAD_COUNT // KEY_VALUE_HEADS
    attention_layer_input = lowered_precision(rms_norm(sequence, norm_one))
    query_raw = lowered_backward(matrix_product(attention_layer_input, query_weight)).reshape(sequence_length, QUERY_HEAD_COUNT, HEAD_SIZE)
    key_unrotated = lowered_backward(matrix_product(attention_layer_input, key_matrix)).reshape(sequence_length, KEY_VALUE_HEADS, HEAD_SIZE)
    value_lowered = lowered_precision(lowered_backward(matrix_product(attention_layer_input, value_matrix))).reshape(sequence_length, KEY_VALUE_HEADS, HEAD_SIZE)
    cosine, sine = rope_tables(sequence_length)
    query_rotated = lowered_precision(rotary(rms_norm(query_raw, query_norm), cosine, sine))
    key_rot = lowered_precision(rotary(rms_norm(key_unrotated, key_norm), cosine, sine))
    block_slice = min(512, sequence_length)
    item_count = sequence_length // block_slice
    block_list = query_rotated.reshape(item_count, block_slice, KEY_VALUE_HEADS, head_ratio, HEAD_SIZE)
    starts = jnp.arange(item_count).astype(jnp.int32) * block_slice
    mixed = lax.map(jax.checkpoint(lambda item: attend_block(item[0], item[1], key_rot, value_lowered)), (block_list, starts))
    mixed = mixed.reshape(sequence_length, QUERY_HEAD_COUNT * HEAD_SIZE)
    residual = sequence + lowered_backward(matrix_product(mixed, output_weight))
    ffn_input = lowered_precision(rms_norm(residual, norm_two))
    gate = lowered_backward(matrix_product(ffn_input, gate_weight))
    up_part = lowered_backward(matrix_product(ffn_input, up_weight))
    hidden = lowered_precision(jax.nn.silu(gate) * up_part)
    return residual + lowered_backward(matrix_product(hidden, down_weight))

def reference(layer_input, attention_norm, query_weight, key_matrix, value_matrix, query_norm, key_norm, output_weight, feedforward_norm, gate_weight, up_weight, down_weight, out_grad):
    params = (attention_norm.astype(jnp.float32), query_weight.astype(jnp.float32), key_matrix.astype(jnp.float32), value_matrix.astype(jnp.float32), query_norm.astype(jnp.float32), key_norm.astype(jnp.float32), output_weight.astype(jnp.float32), feedforward_norm.astype(jnp.float32), gate_weight.astype(jnp.float32), up_weight.astype(jnp.float32), down_weight.astype(jnp.float32))
    sequences = layer_input.astype(jnp.float32).reshape(SEQS, SEQ_LEN, MODEL_WIDTH)

    def whole(seq_all, weights):
        return lax.map(jax.checkpoint(lambda one: layer_sequence(one, weights)), seq_all)
    output, pull = jax.vjp(whole, sequences, params)
    grad_in, grads = pull(out_grad.astype(jnp.float32).reshape(SEQS, SEQ_LEN, MODEL_WIDTH))
    return (output.reshape(TOKENS, MODEL_WIDTH).astype(jnp.bfloat16), grad_in.reshape(TOKENS, MODEL_WIDTH), grads[0], grads[1], grads[2], grads[3], grads[4], grads[5], grads[6], grads[7], grads[8], grads[9], grads[10])
```

```python
import functools
import math

import jax
import jax.numpy as jnp
from jax import lax
from jax.experimental import pallas as pl
from jax.experimental.pallas import tpu as pltpu
from jax.sharding import PartitionSpec as P

HEAD_SIZE = 128
SEQ_LEN = 2048
BLOCK_Q = 512
BLOCK_K = 512

epsilon = 1e-06
rope_base = 1000000.0
scale = HEAD_SIZE ** (-0.5)
log2_e = math.log2(math.e)
axes = ("dp", "tensor")
bf16 = jnp.bfloat16
f32 = jnp.float32
VMEM_LIMIT = 60 * 1024 * 1024


def params(n):
    return pltpu.CompilerParams(
        dimension_semantics=("arbitrary",) * n, vmem_limit_bytes=VMEM_LIMIT
    )


def cost(flops, nbytes, trans=0):
    return pl.CostEstimate(
        flops=int(flops), bytes_accessed=int(nbytes), transcendentals=int(trans)
    )


def contract(left, right, left_dim, right_dim):
    return lax.dot_general(
        left, right, (((left_dim,), (right_dim,)), ((), ())), preferred_element_type=f32
    )


def rms_norm(values, gain):
    return values * lax.rsqrt(jnp.mean(values * values, axis=-1, keepdims=True) + epsilon) * gain


def norm_backward(values, gain, grad):
    inverse = lax.rsqrt(jnp.mean(values * values, axis=-1, keepdims=True) + epsilon)
    normed = values * inverse
    inner = grad * gain
    back = inverse * (inner - normed * jnp.mean(inner * normed, axis=-1, keepdims=True))
    return back, jnp.sum(grad * normed, axis=0)


def rope_tables():
    row = lax.optimization_barrier(jnp.arange(SEQ_LEN).astype(f32))
    inverse = jnp.power(
        rope_base, -jnp.arange(HEAD_SIZE // 2).astype(f32) * (2.0 / HEAD_SIZE)
    )
    angles = row[:, None] * inverse[None, :]
    cosine, sine = jnp.cos(angles), jnp.sin(angles)
    return (
        jnp.concatenate([cosine, cosine], axis=-1),
        jnp.concatenate([-sine, sine], axis=-1),
    )


def project_kernel(nq, nkv, x_ref, w_ref, qg_ref, kg_ref, cos_ref, sin_ref,
                   raw_ref, q_ref, k_ref, v_ref):
    x = x_ref[...]
    cosine, sine = cos_ref[...], sin_ref[...]
    heads = nq + 2 * nkv
    step = 2 if heads % 2 == 0 else 1
    for base in range(0, heads, step):
        both = jnp.dot(
            x, w_ref[:, base * 128:(base + step) * 128], preferred_element_type=f32
        )
        for h in range(base, base + step):
            u = both[:, (h - base) * 128:(h - base + 1) * 128]
            if h >= nq + nkv:
                at = h - nq - nkv
                v_ref[:, at * 128:(at + 1) * 128] = u.astype(bf16)
                continue
            raw_ref[:, h * 128:(h + 1) * 128] = u
            gain = qg_ref[...] if h < nq else kg_ref[...]
            inverse = lax.rsqrt(jnp.mean(u * u, axis=-1, keepdims=True) + epsilon)
            n = u * inverse * gain
            rot = (n * cosine + pltpu.roll(n, 64, 1) * sine).astype(bf16)
            if h < nq:
                q_ref[:, h * 128:(h + 1) * 128] = rot
            else:
                k_ref[:, (h - nq) * 128:(h - nq + 1) * 128] = rot


def project(x, w, query_norm, key_norm, cosine, sine, nq, nkv):
    rows, width = x.shape
    bm = 256
    per_seq = SEQ_LEN // bm
    heads = nq + 2 * nkv
    return pl.pallas_call(
        functools.partial(project_kernel, nq, nkv),
        name="project",
        grid=(rows // bm,),
        in_specs=[
            pl.BlockSpec((bm, width), lambda i: (i, 0)),
            pl.BlockSpec((width, heads * 128), lambda i: (0, 0)),
            pl.BlockSpec((1, 128), lambda i: (0, 0)),
            pl.BlockSpec((1, 128), lambda i: (0, 0)),
            pl.BlockSpec((bm, 128), lambda i: (i % per_seq, 0)),
            pl.BlockSpec((bm, 128), lambda i: (i % per_seq, 0)),
        ],
        out_specs=[
            pl.BlockSpec((bm, (nq + nkv) * 128), lambda i: (i, 0)),
            pl.BlockSpec((bm, nq * 128), lambda i: (i, 0)),
            pl.BlockSpec((bm, nkv * 128), lambda i: (i, 0)),
            pl.BlockSpec((bm, nkv * 128), lambda i: (i, 0)),
        ],
        out_shape=[
            jax.ShapeDtypeStruct((rows, (nq + nkv) * 128), f32),
            jax.ShapeDtypeStruct((rows, nq * 128), bf16),
            jax.ShapeDtypeStruct((rows, nkv * 128), bf16),
            jax.ShapeDtypeStruct((rows, nkv * 128), bf16),
        ],
        compiler_params=params(1),
        cost_estimate=cost(2 * rows * width * heads * 128, rows * width * 10),
    )(x, w, query_norm.reshape(1, 128), key_norm.reshape(1, 128), cosine, sine)


def nt(left, right):
    return contract(left, right, 1, 1)


def forward_kernel(group, bq, bk, q_ref, k_ref, v_ref, o_ref, lse_ref, vone_ref, acc_ref):
    i = pl.program_id(1)

    @pl.when(i == 0)
    def _():
        vone_ref[:, :128] = v_ref[...]
        vone_ref[:, 128:] = jnp.ones_like(v_ref)

    factor = scale * log2_e

    def tile(j, masked, first):
        keys = k_ref[pl.ds(pl.multiple_of(j * bk, bk), bk), :]
        values = vone_ref[pl.ds(pl.multiple_of(j * bk, bk), bk), :]
        for g in range(group):
            s = nt(q_ref[:, g * 128:(g + 1) * 128], keys) * factor
            if masked:
                row = lax.broadcasted_iota(jnp.int32, (bq, bk), 0)
                col = lax.broadcasted_iota(jnp.int32, (bq, bk), 1)
                s = jnp.where(col <= row, s, -1e30)
            p = jnp.exp2(s).astype(bf16)
            part = jnp.dot(p, values, preferred_element_type=f32)
            if first:
                acc_ref[g] = part
            else:
                acc_ref[g] += part

    tile(i, True, True)

    def body(j, carry):
        tile(j, False, False)
        return carry

    lax.fori_loop(0, i, body, 0)
    for g in range(group):
        total = acc_ref[g, :, 128:]
        o_ref[:, g * 128:(g + 1) * 128] = (acc_ref[g, :, :128] / total).astype(bf16)
        logs = jnp.log(total) * log2_e
        lse_ref[0, g:g + 1, :] = logs.T[0:1, :]


def attend_forward(q, k, v, nq, nkv):
    rows = q.shape[0]
    seqs = rows // SEQ_LEN
    group = nq // nkv
    bq = bk = min(BLOCK_Q, SEQ_LEN)
    blocks = SEQ_LEN // bq
    half = rows * SEQ_LEN * nq * 128 * 1.25
    return pl.pallas_call(
        functools.partial(forward_kernel, group, bq, bk),
        name="attend_forward",
        grid=(seqs * nkv, blocks),
        in_specs=[
            pl.BlockSpec((bq, group * 128), lambda h, i: ((h // nkv) * blocks + i, h % nkv)),
            pl.BlockSpec((SEQ_LEN, 128), lambda h, i: (h // nkv, h % nkv)),
            pl.BlockSpec((SEQ_LEN, 128), lambda h, i: (h // nkv, h % nkv)),
        ],
        out_specs=[
            pl.BlockSpec((bq, group * 128), lambda h, i: ((h // nkv) * blocks + i, h % nkv)),
            pl.BlockSpec((1, group, bq), lambda h, i: (h, 0, i)),
        ],
        out_shape=[
            jax.ShapeDtypeStruct((rows, nq * 128), bf16),
            jax.ShapeDtypeStruct((seqs * nkv, group, SEQ_LEN), f32),
        ],
        scratch_shapes=[
            pltpu.VMEM((SEQ_LEN, 256), bf16),
            pltpu.VMEM((group, bq, 256), f32),
        ],
        compiler_params=params(2),
        cost_estimate=cost(2 * half, rows * nq * 128 * 6, rows * SEQ_LEN * nq // 2),
    )(q, k, v)


def unrotate(grad, cosine, sine):
    return grad * cosine - pltpu.roll(grad, 64, 1) * sine


def head_norm_backward(grad, raw, gain):
    inverse = lax.rsqrt(jnp.mean(raw * raw, axis=-1, keepdims=True) + epsilon)
    n = raw * inverse
    inner = grad * gain
    back = inverse * (inner - n * jnp.mean(inner * n, axis=-1, keepdims=True))
    return back, jnp.sum(grad * n, axis=0, keepdims=True)


def backward_kernel(group, bq, bk, blocks, q_ref, do_ref, o_ref, lse_ref, k_ref, v_ref,
                    qraw_ref, kraw_ref, cosb_ref, sinb_ref, cos_ref, sin_ref,
                    qg_ref, kg_ref,
                    dq_ref, dk_ref, dv_ref, gq_ref, gk_ref,
                    dkacc_ref, dvacc_ref, dqacc_ref):
    h, i = pl.program_id(0), pl.program_id(1)

    @pl.when(jnp.logical_and(h == 0, i == 0))
    def _():
        gq_ref[...] = jnp.zeros_like(gq_ref)
        gk_ref[...] = jnp.zeros_like(gk_ref)

    @pl.when(i == 0)
    def _():
        dkacc_ref[...] = jnp.zeros_like(dkacc_ref)
        dvacc_ref[...] = jnp.zeros_like(dvacc_ref)

    factor = scale * log2_e
    deltas = []
    for g in range(group):
        cols = slice(g * 128, (g + 1) * 128)
        both = do_ref[:, cols].astype(f32) * o_ref[:, cols].astype(f32)
        deltas.append(jnp.sum(both.T, axis=0, keepdims=True))

    def tile(j, masked, first):
        at = pl.ds(pl.multiple_of(j * bk, bk), bk)
        keys, values = k_ref[at, :], v_ref[at, :]
        for g in range(group):
            cols = slice(g * 128, (g + 1) * 128)
            q, do = q_ref[:, cols], do_ref[:, cols]
            s = nt(keys, q) * factor - lse_ref[0, g:g + 1, :]
            if masked:
                row = lax.broadcasted_iota(jnp.int32, (bk, bq), 0)
                col = lax.broadcasted_iota(jnp.int32, (bk, bq), 1)
                s = jnp.where(row <= col, s, -1e30)
            p = jnp.exp2(s)
            dp = nt(values, do)
            ds = (p * (dp - deltas[g])).astype(bf16)
            dvacc_ref[at, :] += jnp.dot(p.astype(bf16), do, preferred_element_type=f32)
            dkacc_ref[at, :] += jnp.dot(ds, q, preferred_element_type=f32)
            part = contract(ds, keys, 0, 0)
            if first:
                dqacc_ref[g] = part
            else:
                dqacc_ref[g] += part

    tile(i, True, True)

    def body(j, carry):
        tile(j, False, False)
        return carry

    lax.fori_loop(0, i, body, 0)
    cosine, sine = cosb_ref[...], sinb_ref[...]
    for g in range(group):
        cols = slice(g * 128, (g + 1) * 128)
        grad = unrotate(dqacc_ref[g] * scale, cosine, sine)
        back, gain_grad = head_norm_backward(grad, qraw_ref[:, cols], qg_ref[...])
        dq_ref[:, cols] = back.astype(bf16)
        gq_ref[...] += gain_grad

    @pl.when(i == blocks - 1)
    def _():
        for b in range(blocks):
            rows = slice(b * bq, (b + 1) * bq)
            grad = unrotate(dkacc_ref[rows, :] * scale, cos_ref[rows, :], sin_ref[rows, :])
            back, gain_grad = head_norm_backward(grad, kraw_ref[rows, :], kg_ref[...])
            dk_ref[rows, :] = back.astype(bf16)
            gk_ref[...] += gain_grad
        dv_ref[...] = dvacc_ref[...].astype(bf16)


def attend_backward(q, k, v, do, o, lse, raw, cosine, sine, query_norm, key_norm, nq, nkv):
    rows = q.shape[0]
    seqs = rows // SEQ_LEN
    group = nq // nkv
    bq = bk = min(BLOCK_Q, SEQ_LEN)
    blocks = SEQ_LEN // bq
    half = rows * SEQ_LEN * nq * 128 * 1.25
    q_spec = pl.BlockSpec((bq, group * 128), lambda h, i: ((h // nkv) * blocks + i, h % nkv))
    kv_spec = pl.BlockSpec((SEQ_LEN, 128), lambda h, i: (h // nkv, h % nkv))
    gain_spec = pl.BlockSpec((1, 128), lambda h, i: (0, 0))
    table = pl.BlockSpec((SEQ_LEN, 128), lambda h, i: (0, 0))
    return pl.pallas_call(
        functools.partial(backward_kernel, group, bq, bk, blocks),
        name="attend_backward",
        grid=(seqs * nkv, blocks),
        in_specs=[
            q_spec, q_spec, q_spec,
            pl.BlockSpec((1, group, bq), lambda h, i: (h, 0, i)),
            kv_spec, kv_spec,
            q_spec,
            pl.BlockSpec((SEQ_LEN, 128), lambda h, i: (h // nkv, nq + h % nkv)),
            pl.BlockSpec((bq, 128), lambda h, i: (i, 0)),
            pl.BlockSpec((bq, 128), lambda h, i: (i, 0)),
            table, table, gain_spec, gain_spec,
        ],
        out_specs=[q_spec, kv_spec, kv_spec, gain_spec, gain_spec],
        out_shape=[
            jax.ShapeDtypeStruct((rows, nq * 128), bf16),
            jax.ShapeDtypeStruct((rows, nkv * 128), bf16),
            jax.ShapeDtypeStruct((rows, nkv * 128), bf16),
            jax.ShapeDtypeStruct((1, 128), f32),
            jax.ShapeDtypeStruct((1, 128), f32),
        ],
        scratch_shapes=[
            pltpu.VMEM((SEQ_LEN, 128), f32),
            pltpu.VMEM((SEQ_LEN, 128), f32),
            pltpu.VMEM((group, bq, 128), f32),
        ],
        compiler_params=params(2),
        cost_estimate=cost(5 * half, rows * nq * 128 * 16, rows * SEQ_LEN * nq // 2),
    )(q, do, o, lse, k, v, raw, raw, cosine, sine, cosine, sine,
      query_norm.reshape(1, 128), key_norm.reshape(1, 128))


def gated_kernel(fw, x_ref, g_ref, wgu_ref, wd_ref, hidden_ref, gu_ref):
    x = x_ref[...]
    gate = jnp.dot(x, wgu_ref[:, :fw], preferred_element_type=f32)
    up = jnp.dot(x, wgu_ref[:, fw:], preferred_element_type=f32)
    grad = jnp.dot(g_ref[...], wd_ref[...], preferred_element_type=f32)
    sig = jax.nn.sigmoid(gate)
    silu = gate * sig
    hidden_ref[...] = (silu * up).astype(bf16)
    gu_ref[:, :fw] = (grad * up * (sig * (1.0 + gate * (1.0 - sig)))).astype(bf16)
    gu_ref[:, fw:] = (grad * silu).astype(bf16)


def gated(x, grad, w2, ffl, fw):
    rows, width = x.shape
    bm = 512
    n = ffl // fw
    return pl.pallas_call(
        functools.partial(gated_kernel, fw),
        name="gated",
        grid=(n, rows // bm),
        in_specs=[
            pl.BlockSpec((bm, width), lambda j, i: (i, 0)),
            pl.BlockSpec((bm, width), lambda j, i: (i, 0)),
            pl.BlockSpec((width, 2 * fw), lambda j, i: (0, j)),
            pl.BlockSpec((width, fw), lambda j, i: (0, 2 * n + j)),
        ],
        out_specs=[
            pl.BlockSpec((bm, fw), lambda j, i: (i, j)),
            pl.BlockSpec((bm, 2 * fw), lambda j, i: (i, j)),
        ],
        out_shape=[
            jax.ShapeDtypeStruct((rows, ffl), bf16),
            jax.ShapeDtypeStruct((rows, 2 * ffl), bf16),
        ],
        compiler_params=params(2),
        cost_estimate=cost(6 * rows * width * ffl, rows * ffl * 6, rows * ffl),
    )(x, grad, w2, w2)


class Swapped:
    def __init__(self, dp):
        pairs = dp // 2
        at = lambda k, c, t: (k * 2 + c) * 2 + t
        every = [(k, c, t) for k in range(pairs) for c in range(2) for t in range(2)]
        self.trade = [(at(k, c, t), at(k, t, c)) for k, c, t in every]
        self.other = [(at(k, c, t), at(k, 1 - c, t)) for k, c, t in every]
        self.groups = [[at(k, c, t) for k in range(pairs) for t in range(2)] for c in range(2)]

    def place(self):
        return lax.rem(lax.axis_index("dp"), 2)

    def move(self, x):
        return lax.ppermute(x, axes, self.trade)

    def gather(self, x):
        return lax.all_gather(x, axes, axis=0, tiled=True, axis_index_groups=self.groups)

    def scatter(self, x):
        return lax.psum_scatter(
            x, axes, scatter_dimension=0, tiled=True, axis_index_groups=self.groups
        )

    def join(self, x):
        peer = lax.ppermute(x, axes, self.other)
        first = self.place() == 0
        return jnp.concatenate([jnp.where(first, x, peer), jnp.where(first, peer, x)], axis=0)

    def reduce(self, left, product):
        rows = left.shape[0] // 2
        mine = self.place() * rows
        theirs = rows - mine
        away = product(lax.dynamic_slice_in_dim(left, theirs, rows)).astype(bf16)
        come = lax.ppermute(away, axes, self.other)
        return product(lax.dynamic_slice_in_dim(left, mine, rows)) + come.astype(f32)


class Plain:
    def move(self, x):
        return x

    def gather(self, x):
        return lax.all_gather(x, "dp", axis=0, tiled=True)

    def scatter(self, x):
        return lax.psum_scatter(x, "dp", scatter_dimension=0, tiled=True)

    def join(self, x):
        return lax.all_gather(x, "tensor", axis=0, tiled=True)

    def reduce(self, left, product):
        return lax.psum_scatter(
            product(left).astype(bf16), "tensor", scatter_dimension=0, tiled=True
        ).astype(f32)


def on_device(
    plan,
    layer_input,
    attention_norm,
    query_weight,
    key_matrix,
    value_matrix,
    query_norm,
    key_norm,
    output_weight,
    feedforward_norm,
    gate_weight,
    up_weight,
    down_weight,
    out_grad,
):
    nq = query_weight.shape[1] // HEAD_SIZE
    nkv = key_matrix.shape[1] // HEAD_SIZE
    shard = query_weight.shape[0]
    ffl = gate_weight.shape[1]
    fw = 512 if ffl % 512 == 0 else ffl
    chunks = ffl // fw

    first_pack = jnp.concatenate([query_weight, key_matrix, value_matrix], axis=1)
    w1 = plan.gather(plan.move(first_pack))
    tokens = plan.move(layer_input)
    interleaved = jnp.stack(
        [gate_weight.reshape(shard, chunks, fw), up_weight.reshape(shard, chunks, fw)], axis=2
    ).reshape(shard, 2 * ffl)
    second_pack = jnp.concatenate([interleaved, down_weight.T, output_weight.T], axis=1)
    w2 = plan.gather(plan.move(second_pack))
    cotangent = plan.move(out_grad)

    cosine, sine = rope_tables()
    input_float = tokens.astype(f32)
    attention_all = plan.join(rms_norm(input_float, attention_norm).astype(bf16))
    grad_all = plan.join(cotangent)
    raw, q, k, v = project(attention_all, w1, query_norm, key_norm, cosine, sine, nq, nkv)
    mixed, lse = attend_forward(q, k, v, nq, nkv)
    w_out = w2[:, 3 * ffl:]
    residual = input_float + plan.reduce(mixed, lambda m: contract(m, w_out, 1, 1))
    ffn_all = plan.join(rms_norm(residual, feedforward_norm).astype(bf16))
    hidden, gu = gated(ffn_all, grad_all, w2, ffl, fw)
    ffn_input_grad = plan.reduce(gu, lambda m: contract(m, w2[:, :2 * ffl], 1, 1))
    norm_two_back, norm_two_grad = norm_backward(residual, feedforward_norm, ffn_input_grad)
    residual_grad = cotangent.astype(f32) + norm_two_back
    proj_all = plan.join(residual_grad.astype(bf16))
    ffn_parts = jnp.concatenate(
        [
            contract(ffn_all, gu, 0, 0).astype(bf16),
            contract(grad_all, hidden, 0, 0).astype(bf16),
            contract(proj_all, mixed, 0, 0).astype(bf16),
        ],
        axis=1,
    )
    second_grad = plan.move(plan.scatter(ffn_parts))
    mixed_grad = contract(proj_all, w_out, 1, 0).astype(bf16)
    layer_sum = residual + plan.reduce(
        hidden, lambda m: contract(m, w2[:, 2 * ffl:3 * ffl], 1, 1)
    )
    layer_output = plan.move(layer_sum.astype(bf16))
    dq, dk, dv, query_norm_part, key_norm_part = attend_backward(
        q, k, v, mixed_grad, mixed, lse, raw, cosine, sine, query_norm, key_norm, nq, nkv
    )
    bits = jnp.concatenate([dq, dk, dv], axis=1)
    first_grad = plan.move(plan.scatter(contract(attention_all, bits, 0, 0).astype(bf16)))
    attention_input_grad = plan.reduce(bits, lambda m: contract(m, w1, 1, 1))
    norm_one_back, norm_one_grad = norm_backward(
        input_float, attention_norm, attention_input_grad
    )
    input_grad = plan.move((residual_grad + norm_one_back).astype(bf16)).astype(f32)
    sums = lax.psum(
        jnp.concatenate(
            [norm_one_grad, norm_two_grad, query_norm_part[0], key_norm_part[0]]
        ),
        axes,
    )
    width = attention_norm.shape[0]
    q_cols, kv_cols = nq * HEAD_SIZE, nkv * HEAD_SIZE
    first_grad = first_grad.astype(f32)
    second_grad = second_grad.astype(f32)
    pairs = second_grad[:, :2 * ffl].reshape(shard, chunks, 2, fw)
    return (
        layer_output,
        input_grad,
        sums[:width],
        first_grad[:, :q_cols],
        first_grad[:, q_cols:q_cols + kv_cols],
        first_grad[:, q_cols + kv_cols:],
        sums[2 * width:2 * width + HEAD_SIZE],
        sums[2 * width + HEAD_SIZE:],
        second_grad[:, 3 * ffl:].T,
        sums[width:2 * width],
        pairs[:, :, 0].reshape(shard, ffl),
        pairs[:, :, 1].reshape(shard, ffl),
        second_grad[:, 2 * ffl:3 * ffl].T,
    )


def solution(mesh):
    dp, tensor = mesh.shape["dp"], mesh.shape["tensor"]
    plan = Swapped(dp) if tensor == 2 and dp % 2 == 0 else Plain()
    return jax.shard_map(
        functools.partial(on_device, plan),
        mesh=mesh,
        in_specs=(
            P(("dp", "tensor"), None),
            P(),
            P("dp", "tensor"),
            P("dp", "tensor"),
            P("dp", "tensor"),
            P(),
            P(),
            P("tensor", "dp"),
            P(),
            P("dp", "tensor"),
            P("dp", "tensor"),
            P("tensor", "dp"),
            P(("dp", "tensor"), None),
        ),
        out_specs=(
            P(("dp", "tensor"), None),
            P(("dp", "tensor"), None),
            P(),
            P("dp", "tensor"),
            P("dp", "tensor"),
            P("dp", "tensor"),
            P(),
            P(),
            P("tensor", "dp"),
            P(),
            P("dp", "tensor"),
            P("dp", "tensor"),
            P("tensor", "dp"),
        ),
        check_vma=False,
    )
```
